512 devices in a mesh: pipe: 4 (over z_hi, core), seq: 128 (over y, x, z_lo).
Axes of the slice: x: 4, y: 8, z: 8 (z_hi: 2, z_lo: 4; z = z_hi * 4 + z_lo), core: 2. Of those that a mesh axis runs over, the one named last changes fastest.
Arguments:
- layer_input: bfloat16 [4, 16384, 256], P('pipe', 'seq'), may hold values from -6 to 6
- filters: float32 [4, 16384, 256], P('pipe', 'seq'), may hold values from -1 to 1
- skip: float32 [4, 256], P('pipe'), may hold values from 0.5 to 1.5
- incoming: bfloat16 [4, 16384, 256], P('pipe', 'seq'), may hold values from -6 to 6
- loss_grad: bfloat16 [16384, 256], P('seq'), may hold values from -6 to 6
Outputs:
- input_grad: bfloat16 [4, 16384, 256], P('pipe', 'seq')
- filter_grad: float32 [4, 16384, 256], P('pipe', 'seq')
The draws below stay inside these ranges and needn't reach their ends.
All inputs are finite; a program needn't handle non-finite values.
Results may differ from the reference program's by a relative error of at most 0.001.
Values may be sent and summed in bfloat16 or wider, within the bound.
No kernel may reach another device: no remote copies, remote signals or barrier semaphores. Data moves between devices by JAX's collectives and lax.ppermute only.
A program may use at most 64 MiB of HBM per device.

```python
import math
import jax
import jax.numpy as jnp
from jax import lax

CHAN = 256
SECTIONS = 4
SEQ = 16384


def draw_filters(key, part):
    key_rate = jax.random.fold_in(key, 11)
    key_noise = jax.random.fold_in(key, 12)
    log_rate = jax.random.uniform(key_rate, (SECTIONS, 1, CHAN), jnp.float32, math.log(0.5), math.log(SEQ / 40.0))
    rate = jnp.exp(log_rate)
    where_pos = lax.broadcasted_iota(jnp.int32, (1, SEQ, 1), 1).astype(jnp.float32) / SEQ
    window = jnp.exp(-rate * where_pos)
    energy = (1.0 - jnp.exp(-2.0 * rate)) / (1.0 - jnp.exp(-2.0 * rate / SEQ))
    noise = jax.random.truncated_normal(key_noise, -4.0, 4.0, (SECTIONS, SEQ, CHAN), jnp.float32)
    return noise * window / jnp.sqrt(energy)


def steps_of(stream_key, dims, pieces, low, top_value):
    level = 1.0
    for dim, parts in pieces:
        steps = jax.random.uniform(jax.random.fold_in(jax.random.fold_in(stream_key, 6), dim), (parts,), jnp.float32, low / len(pieces), top_value / len(pieces))
        level = level * jnp.repeat(jnp.exp(steps), dims[dim] // parts).reshape((-1,) + (1,) * (len(dims) - 1 - dim))
    return level


def scatter_about(own_key, shape, width, most, shards=(), kind=jnp.bfloat16):
    level = steps_of(own_key, shape, shards, -0.22, 0.18) if shards else 1.0
    result = jax.random.normal(own_key, shape, jnp.float32) * width * level
    return jnp.minimum(jnp.maximum(result, -most), most).astype(kind)


def setup_inputs(seed: int = 0) -> dict:
    key_of = jax.random.split(jax.random.key(seed), 6)
    return {
        "layer_input": scatter_about(key_of[0], (SECTIONS, SEQ, CHAN), 1.0, 6.0, ((0, 4), (1, 128))),
        "filters": draw_filters(jax.random.fold_in(key_of[5], 71), 0),
        "skip": jnp.clip(0.5 + 1.0 * jax.random.uniform(key_of[2], (SECTIONS, CHAN), jnp.float32) ** steps_of(key_of[2], (SECTIONS, CHAN), ((0, 4),), -0.2, 0.2), 0.5, 1.5),
        "incoming": scatter_about(key_of[3], (SECTIONS, SEQ, CHAN), 1.0, 6.0, ((0, 4), (1, 128))),
        "loss_grad": scatter_about(key_of[4], (SEQ, CHAN), 1.0, 6.0, ((0, 128),)),
    }


def section_grads(inputs, filt, grad_out, gain):
    size = 2 * SEQ
    u_spec = jnp.fft.rfft(inputs.astype(jnp.float32), n=size, axis=0)
    h_spec = jnp.fft.rfft(filt, n=size, axis=0)
    d_spec = jnp.fft.rfft(grad_out.astype(jnp.float32), n=size, axis=0)
    conv_grad = jnp.fft.irfft(jnp.conj(h_spec) * d_spec, n=size, axis=0)[:SEQ]
    filt_grad = jnp.fft.irfft(d_spec * jnp.conj(u_spec), n=size, axis=0)[:SEQ] * (1.0 / math.sqrt(SEQ))
    input_grad = (conv_grad + gain[None, :] * grad_out.astype(jnp.float32)).astype(jnp.bfloat16)
    return (input_grad, filt_grad.astype(jnp.float32))

def reference(layer_input, filters, skip, incoming, loss_grad):
    grads = []
    filt_grads = []
    for section in range(SECTIONS):
        if section + 1 < SECTIONS:
            grad_out = incoming[section + 1]
        else:
            grad_out = loss_grad
        one_grad, one_filt = section_grads(layer_input[section], filters[section], grad_out, skip[section])
        grads.append(one_grad)
        filt_grads.append(one_filt)
    return (jnp.stack(grads), jnp.stack(filt_grads))
```

```python
import math

import jax
import jax.numpy as jnp
import numpy as np
from jax import lax
from jax.experimental import pallas as pl
from jax.experimental.pallas import tpu as pltpu
from jax.sharding import PartitionSpec as P

BF16 = jnp.bfloat16
F32 = jnp.float32
BLOCK = 128
LENGTH = BLOCK * BLOCK
ROWS = 8
VMEM = pl.BlockSpec(memory_space=pltpu.VMEM)
SMEM = pl.BlockSpec(memory_space=pltpu.SMEM)


def halves(table):
    high = table.astype(BF16)
    low = (table - high.astype(np.float64)).astype(BF16)
    return (high, low)


def tables():
    q = np.arange(BLOCK)
    first = 2.0 * math.pi * np.outer(q + 0.25, q) / BLOCK
    twist = 2.0 * math.pi * np.outer(q + 0.25, q) / LENGTH
    second = 2.0 * math.pi * (np.outer(q, q) % BLOCK) / BLOCK
    gather = np.concatenate([np.cos(first), -np.sin(first)], axis=0)
    turn_re = np.tile(np.cos(twist), (1, 2)).astype(np.float32)
    turn_im = np.tile(-np.sin(twist), (1, 2)).astype(np.float32)
    cos, sin = (np.cos(second), -np.sin(second))
    mix = np.block([[cos, sin], [-sin, cos]])
    spread = gather.T / LENGTH
    return (halves(gather), (turn_re, turn_im), halves(mix), halves(mix.T), halves(spread))


def split(value):
    high = value.astype(BF16)
    return (high, (value - high.astype(F32)).astype(BF16))


def dot(left, right):
    return jnp.dot(left, right, preferred_element_type=F32)


def dot3(left, right):
    return dot(left[0], right[0]) + dot(left[0], right[1]) + dot(left[1], right[0])


def pack_kernel(where_ref, x_ref, f_ref, skip_ref, inc_ref, loss_ref, out_ref, rows_ref):
    at_start = jnp.where(where_ref[0] == 0, 1.0, 0.0)
    row = lax.broadcasted_iota(jnp.int32, (BLOCK, BLOCK), 0)
    first_row = jnp.where(row == 0, at_start, 0.0)
    use_loss = where_ref[1] == 0
    for half in range(2):
        lanes = slice(half * BLOCK, (half + 1) * BLOCK)
        rows_ref[pl.ds(half, BLOCK, stride=ROWS), :] = x_ref[:, lanes].astype(F32).T
        taps = f_ref[:, lanes] + first_row * skip_ref[:, lanes]
        high = taps.astype(BF16).astype(F32)
        rows_ref[pl.ds(2 + half, BLOCK, stride=ROWS), :] = high.T
        rows_ref[pl.ds(4 + half, BLOCK, stride=ROWS), :] = (taps - high).T
        grad = jnp.where(use_loss, loss_ref[:, lanes].astype(F32), inc_ref[:, lanes].astype(F32))
        rows_ref[pl.ds(6 + half, BLOCK, stride=ROWS), :] = grad.T
    out_ref[...] = rows_ref[...].astype(BF16)


def part_kernel(in_ref, own_ref, grad_ref, rows_ref):
    rows_ref[...] = in_ref[...].astype(F32)
    for r in range(6):
        own_ref[:, r * BLOCK : (r + 1) * BLOCK] = rows_ref[pl.ds(r, BLOCK, stride=ROWS), :].astype(BF16)
    for r in range(2):
        grad_ref[:, r * BLOCK : (r + 1) * BLOCK] = rows_ref[pl.ds(6 + r, BLOCK, stride=ROWS), :].astype(BF16)


def to_spectrum(high, low, gather, turn, mix):
    part = dot(gather[0], high) + dot(gather[1], high)
    if low is not None:
        part = part + dot(gather[0], low)
    real, imag = (part[:BLOCK], part[BLOCK:])
    turned_re = real * turn[0] - imag * turn[1]
    turned_im = real * turn[1] + imag * turn[0]
    stacked = jnp.concatenate(
        [
            jnp.concatenate([turned_re[:, :BLOCK], turned_im[:, :BLOCK]], axis=1),
            jnp.concatenate([turned_re[:, BLOCK:], turned_im[:, BLOCK:]], axis=1),
        ],
        axis=0,
    )
    return dot3(split(stacked), mix)


def forward_kernel(own_ref, gh_ref, gl_ref, tr_ref, ti_ref, mh_ref, ml_ref, u_ref, h_ref):
    gather = (gh_ref[...], gl_ref[...])
    turn = (tr_ref[...], ti_ref[...])
    mix = (mh_ref[...], ml_ref[...])
    width = 2 * BLOCK
    u_ref[...] = to_spectrum(own_ref[:, :width], None, gather, turn, mix)
    h_ref[...] = to_spectrum(own_ref[:, width : 2 * width], own_ref[:, 2 * width :], gather, turn, mix)


def back_kernel(
    grad_ref, u_ref, h_ref, gh_ref, gl_ref, tr_ref, ti_ref, mh_ref, ml_ref, bh_ref, bl_ref, sh_ref, sl_ref, out_ref, rows_ref
):
    turn = (tr_ref[...], ti_ref[...])
    grad = to_spectrum(grad_ref[...], None, (gh_ref[...], gl_ref[...]), turn, (mh_ref[...], ml_ref[...]))
    g_re, g_im = (grad[:, :BLOCK], grad[:, BLOCK:])
    back = (bh_ref[...], bl_ref[...])
    spread = (sh_ref[...], sl_ref[...])
    for index, other in enumerate((h_ref, u_ref)):
        o_re, o_im = (other[:, :BLOCK], other[:, BLOCK:])
        product = jnp.concatenate([o_re * g_re + o_im * g_im, o_re * g_im - o_im * g_re], axis=1)
        part = dot3(split(product), back)
        real = jnp.concatenate([part[:BLOCK, :BLOCK], part[BLOCK:, :BLOCK]], axis=1)
        imag = jnp.concatenate([part[:BLOCK, BLOCK:], part[BLOCK:, BLOCK:]], axis=1)
        stacked = jnp.concatenate([real * turn[0] + imag * turn[1], imag * turn[0] - real * turn[1]], axis=0)
        value = dot3(spread, split(stacked))
        for half in range(2):
            one = value[:, half * BLOCK : (half + 1) * BLOCK]
            if index == 0:
                rows_ref[pl.ds(half, BLOCK, stride=ROWS), :] = one
            else:
                one = one * (1.0 / math.sqrt(LENGTH))
                high = one.astype(BF16).astype(F32)
                rows_ref[pl.ds(2 + half, BLOCK, stride=ROWS), :] = high
                rows_ref[pl.ds(4 + half, BLOCK, stride=ROWS), :] = one - high
                rows_ref[pl.ds(6 + half, BLOCK, stride=ROWS), :] = jnp.zeros_like(one)
    out_ref[...] = rows_ref[...].astype(BF16)


def unpack_kernel(in_ref, grad_ref, filt_ref, rows_ref):
    rows_ref[...] = in_ref[...].astype(F32)
    for half in range(2):
        lanes = slice(half * BLOCK, (half + 1) * BLOCK)
        grad_ref[:, lanes] = rows_ref[pl.ds(half, BLOCK, stride=ROWS), :].T.astype(BF16)
        both = rows_ref[pl.ds(2 + half, BLOCK, stride=ROWS), :] + rows_ref[pl.ds(4 + half, BLOCK, stride=ROWS), :]
        filt_ref[:, lanes] = both.T


def shape(rows, columns, kind):
    return jax.ShapeDtypeStruct((rows, columns), kind)


def call(kernel, outs, ins, scratch=()):
    return pl.pallas_call(
        kernel,
        out_shape=outs,
        in_specs=ins,
        out_specs=jax.tree.map(lambda _: VMEM, outs),
        scratch_shapes=scratch,
    )


ROW_SCRATCH = (pltpu.VMEM((ROWS * BLOCK, BLOCK), F32),)
WIDE = 2 * BLOCK


def exchanged(packed):
    blocks = packed.reshape(BLOCK, ROWS, BLOCK)
    blocks = lax.all_to_all(blocks, "seq", split_axis=0, concat_axis=0, tiled=True)
    return blocks.reshape(ROWS * BLOCK, BLOCK)


def per_device(layer_input, filters, skip, incoming, loss_grad):
    gather, turn, mix, back, spread = tables()
    where = jnp.stack([lax.axis_index("seq"), lax.axis_index("pipe")]).astype(jnp.int32)
    packed = call(pack_kernel, shape(ROWS * BLOCK, BLOCK, BF16), [SMEM] + [VMEM] * 5, ROW_SCRATCH)(
        where, layer_input[0], filters[0], skip, incoming[0], loss_grad
    )
    received = exchanged(packed)
    own, grad = call(part_kernel, (shape(BLOCK, 3 * WIDE, BF16), shape(BLOCK, WIDE, BF16)), [VMEM], ROW_SCRATCH)(received)
    parts = lax.axis_size("pipe")
    grad = lax.ppermute(grad, "pipe", [(i, (i - 1) % parts) for i in range(parts)])
    spectrum = shape(WIDE, WIDE, F32)
    forward = (*gather, *turn, *mix)
    u_spec, h_spec = call(forward_kernel, (spectrum, spectrum), [VMEM] * 7)(own, *forward)
    results = call(back_kernel, shape(ROWS * BLOCK, BLOCK, BF16), [VMEM] * 13, ROW_SCRATCH)(
        grad, u_spec, h_spec, *forward, *back, *spread
    )
    arrived = exchanged(results)
    input_grad, filter_grad = call(unpack_kernel, (shape(BLOCK, WIDE, BF16), shape(BLOCK, WIDE, F32)), [VMEM], ROW_SCRATCH)(arrived)
    return (input_grad[None], filter_grad[None])


def solution(mesh):
    return jax.shard_map(
        per_device,
        mesh=mesh,
        in_specs=(
            P("pipe", "seq", None),
            P("pipe", "seq", None),
            P("pipe", None),
            P("pipe", "seq", None),
            P("seq", None),
        ),
        out_specs=(P("pipe", "seq", None), P("pipe", "seq", None)),
        check_vma=False,
    )
```

```python
import math

import jax
import jax.numpy as jnp
import numpy as np
from jax import lax
from jax.experimental import pallas as pl
from jax.experimental.pallas import tpu as pltpu
from jax.sharding import PartitionSpec as P

BF16 = jnp.bfloat16
F32 = jnp.float32
BLOCK = 128
LENGTH = BLOCK * BLOCK
ROWS = 8
VMEM = pl.BlockSpec(memory_space=pltpu.VMEM)
SMEM = pl.BlockSpec(memory_space=pltpu.SMEM)


def halves(table):
    high = table.astype(BF16)
    low = (table - high.astype(np.float64)).astype(BF16)
    return (high, low)


def tables():
    q = np.arange(BLOCK)
    first = 2.0 * math.pi * np.outer(q + 0.25, q) / BLOCK
    twist = 2.0 * math.pi * np.outer(q + 0.25, q) / LENGTH
    second = 2.0 * math.pi * (np.outer(q, q) % BLOCK) / BLOCK
    gather = np.concatenate([np.cos(first), -np.sin(first)], axis=0)
    turn_re = np.tile(np.cos(twist), (1, 2)).astype(np.float32)
    turn_im = np.tile(-np.sin(twist), (1, 2)).astype(np.float32)
    cos, sin = (np.cos(second), -np.sin(second))
    mix = np.block([[cos, sin], [-sin, cos]])
    spread = gather.T / LENGTH
    return (halves(gather), (turn_re, turn_im), halves(mix), halves(mix.T), halves(spread))


def split(value):
    high = value.astype(BF16)
    return (high, (value - high.astype(F32)).astype(BF16))


def dot(left, right):
    return jnp.dot(left, right, preferred_element_type=F32)


def dot3(left, right):
    return dot(left[0], right[0]) + dot(left[0], right[1]) + dot(left[1], right[0])


def pack_kernel(x_ref, f_ref, skip_ref, rows_ref):
    at_start = jnp.where(lax.axis_index("seq") == 0, 1.0, 0.0)
    row = lax.broadcasted_iota(jnp.int32, (BLOCK, BLOCK), 0)
    first_row = jnp.where(row == 0, at_start, 0.0)
    for half in range(2):
        lanes = slice(half * BLOCK, (half + 1) * BLOCK)
        rows_ref[pl.ds(half, BLOCK, stride=ROWS), :] = x_ref[:, lanes].astype(F32).T
        taps = (f_ref[:, lanes] + first_row * skip_ref[:, lanes]).T
        high = taps.astype(BF16).astype(F32)
        rows_ref[pl.ds(2 + half, BLOCK, stride=ROWS), :] = high
        rows_ref[pl.ds(4 + half, BLOCK, stride=ROWS), :] = taps - high


def join_kernel(rows_ref, inc_ref, loss_ref, out_ref, all_ref):
    is_last = lax.axis_index("pipe") == lax.axis_size("pipe") - 1
    all_ref[...] = rows_ref[...]
    for half in range(2):
        lanes = slice(half * BLOCK, (half + 1) * BLOCK)
        grad = jnp.where(is_last, loss_ref[:, lanes].astype(F32), inc_ref[:, lanes].astype(F32))
        all_ref[pl.ds(6 + half, BLOCK, stride=ROWS), :] = grad.T
    out_ref[...] = all_ref[...].astype(BF16)


def to_spectrum(high, low, gather, turn, mix):
    part = dot(gather[0], high) + dot(gather[1], high)
    if low is not None:
        part = part + dot(gather[0], low)
    real, imag = (part[:BLOCK], part[BLOCK:])
    turned_re = real * turn[0] - imag * turn[1]
    turned_im = real * turn[1] + imag * turn[0]
    stacked = jnp.concatenate(
        [
            jnp.concatenate([turned_re[:, :BLOCK], turned_im[:, :BLOCK]], axis=1),
            jnp.concatenate([turned_re[:, BLOCK:], turned_im[:, BLOCK:]], axis=1),
        ],
        axis=0,
    )
    return dot3(split(stacked), mix)


def main_kernel(in_ref, gh_ref, gl_ref, tr_ref, ti_ref, mh_ref, ml_ref, bh_ref, bl_ref, sh_ref, sl_ref, out_ref, rows_ref):
    gather = (gh_ref[...], gl_ref[...])
    turn = (tr_ref[...], ti_ref[...])
    mix = (mh_ref[...], ml_ref[...])
    back = (bh_ref[...], bl_ref[...])
    spread = (sh_ref[...], sl_ref[...])
    rows_ref[...] = in_ref[...].astype(F32)

    def pair(r):
        both = [rows_ref[pl.ds(r + half, BLOCK, stride=ROWS), :].astype(BF16) for half in range(2)]
        return jnp.concatenate(both, axis=1)

    grad = to_spectrum(pair(6), None, gather, turn, mix)
    g_re, g_im = (grad[:, :BLOCK], grad[:, BLOCK:])
    taps = to_spectrum(pair(2), pair(4), gather, turn, mix)
    inputs = to_spectrum(pair(0), None, gather, turn, mix)
    for index, other in enumerate((taps, inputs)):
        o_re, o_im = (other[:, :BLOCK], other[:, BLOCK:])
        product = jnp.concatenate([o_re * g_re + o_im * g_im, o_re * g_im - o_im * g_re], axis=1)
        part = dot3(split(product), back)
        real = jnp.concatenate([part[:BLOCK, :BLOCK], part[BLOCK:, :BLOCK]], axis=1)
        imag = jnp.concatenate([part[:BLOCK, BLOCK:], part[BLOCK:, BLOCK:]], axis=1)
        stacked = jnp.concatenate([real * turn[0] + imag * turn[1], imag * turn[0] - real * turn[1]], axis=0)
        value = dot3(spread, split(stacked))
        for half in range(2):
            one = value[:, half * BLOCK : (half + 1) * BLOCK]
            if index == 0:
                rows_ref[pl.ds(half, BLOCK, stride=ROWS), :] = one
            else:
                one = one * (1.0 / math.sqrt(LENGTH))
                high = one.astype(BF16).astype(F32)
                rows_ref[pl.ds(2 + half, BLOCK, stride=ROWS), :] = high
                rows_ref[pl.ds(4 + half, BLOCK, stride=ROWS), :] = one - high
                rows_ref[pl.ds(6 + half, BLOCK, stride=ROWS), :] = jnp.zeros_like(one)
    out_ref[...] = rows_ref[...].astype(BF16)


def unpack_kernel(in_ref, grad_ref, filt_ref, rows_ref):
    rows_ref[...] = in_ref[...].astype(F32)
    for half in range(2):
        lanes = slice(half * BLOCK, (half + 1) * BLOCK)
        grad_ref[:, lanes] = rows_ref[pl.ds(half, BLOCK, stride=ROWS), :].T.astype(BF16)
        both = rows_ref[pl.ds(2 + half, BLOCK, stride=ROWS), :] + rows_ref[pl.ds(4 + half, BLOCK, stride=ROWS), :]
        filt_ref[:, lanes] = both.T


def shape(rows, columns, kind):
    return jax.ShapeDtypeStruct((rows, columns), kind)


def near(value):
    return pltpu.with_memory_space_constraint(value, pltpu.VMEM)


def call(kernel, outs, ins, scratch=()):
    return pl.pallas_call(
        kernel,
        out_shape=outs,
        in_specs=[VMEM] * ins,
        out_specs=jax.tree.map(lambda _: VMEM, outs),
        scratch_shapes=scratch,
    )


ROW_SCRATCH = (pltpu.VMEM((ROWS * BLOCK, BLOCK), F32),)
PACKED = pltpu.VMEM((ROWS * BLOCK, BLOCK), BF16)
WIDE = 2 * BLOCK


def exchanged(packed):
    blocks = packed.reshape(BLOCK, ROWS, BLOCK)
    blocks = lax.all_to_all(blocks, "seq", split_axis=0, concat_axis=0, tiled=True)
    return near(blocks.reshape(ROWS * BLOCK, BLOCK))


def per_device(layer_input, filters, skip, incoming, loss_grad):
    constants = [near(jnp.asarray(half)) for pair in tables() for half in pair]
    parts = lax.axis_size("pipe")
    passed = lax.ppermute(incoming[0], "pipe", [(i, i - 1) for i in range(1, parts)])
    rows = call(pack_kernel, pltpu.VMEM((ROWS * BLOCK, BLOCK), F32), 3)(layer_input[0], filters[0], skip)
    packed = call(join_kernel, PACKED, 3, ROW_SCRATCH)(near(rows), near(passed), near(loss_grad))
    results = call(main_kernel, PACKED, 11, ROW_SCRATCH)(exchanged(packed), *constants)
    outs = (shape(BLOCK, WIDE, BF16), shape(BLOCK, WIDE, F32))
    input_grad, filter_grad = call(unpack_kernel, outs, 1, ROW_SCRATCH)(exchanged(results))
    return (input_grad[None], filter_grad[None])


def solution(mesh):
    return jax.shard_map(
        per_device,
        mesh=mesh,
        in_specs=(
            P("pipe", "seq", None),
            P("pipe", "seq", None),
            P("pipe", None),
            P("pipe", "seq", None),
            P("seq", None),
        ),
        out_specs=(P("pipe", "seq", None), P("pipe", "seq", None)),
        check_vma=False,
    )
```

```python
import math

import jax
import jax.numpy as jnp
import numpy as np
from jax import lax
from jax.experimental import pallas as pl
from jax.experimental.pallas import tpu as pltpu
from jax.sharding import PartitionSpec as P

BF16 = jnp.bfloat16
F32 = jnp.float32
BLOCK = 128
LENGTH = BLOCK * BLOCK
ROWS = 8
BACK_ROWS = 6
ORDER = [int(f"{i:07b}"[::-1], 2) for i in range(BLOCK)]
VMEM = pl.BlockSpec(memory_space=pltpu.VMEM)
SMEM = pl.BlockSpec(memory_space=pltpu.SMEM)


def halves(table):
    high = table.astype(BF16)
    low = (table - high.astype(np.float64)).astype(BF16)
    return (high, low)


def tables():
    q = np.arange(BLOCK)
    order = np.array(ORDER)
    first = 2.0 * math.pi * np.outer(q + 0.25, order) / BLOCK
    moved = 2.0 * math.pi * np.outer(q + 0.25, order ^ 2) / BLOCK
    twist = 2.0 * math.pi * np.outer(q + 0.25, q) / LENGTH
    second = 2.0 * math.pi * (np.outer(q, q) % BLOCK) / BLOCK
    gather = np.concatenate([np.cos(first), -np.sin(first)], axis=0)
    moved = np.concatenate([np.cos(moved), -np.sin(moved)], axis=0)
    turn_re = np.tile(np.cos(twist), (1, 2)).astype(np.float32)
    turn_im = np.tile(-np.sin(twist), (1, 2)).astype(np.float32)
    cos, sin = (np.cos(second), -np.sin(second))
    mix = np.block([[cos, sin], [-sin, cos]])
    spread = gather.T / LENGTH
    return (halves(gather), halves(moved), (turn_re, turn_im), halves(mix), halves(mix.T), halves(spread))


def split(value):
    high = value.astype(BF16)
    return (high, (value - high.astype(F32)).astype(BF16))


def dot(left, right):
    return jnp.dot(left, right, preferred_element_type=F32)


def dot3(left, right):
    return dot(left[0], right[0]) + dot(left[0], right[1]) + dot(left[1], right[0])


def pack_kernel(x_ref, f_ref, skip_ref, rows_ref):
    at_start = jnp.where(lax.axis_index("seq") == 0, 1.0, 0.0)
    row = lax.broadcasted_iota(jnp.int32, (BLOCK, BLOCK), 0)
    first_row = jnp.where(row == 0, at_start, 0.0)
    for half in range(2):
        lanes = slice(half * BLOCK, (half + 1) * BLOCK)
        rows_ref[pl.ds(half, BLOCK, stride=ROWS), :] = x_ref[:, lanes].astype(F32).T
        taps = (f_ref[:, lanes] + first_row * skip_ref[:, lanes]).T
        high = taps.astype(BF16).astype(F32)
        rows_ref[pl.ds(2 + half, BLOCK, stride=ROWS), :] = high
        rows_ref[pl.ds(4 + half, BLOCK, stride=ROWS), :] = taps - high


def join_kernel(rows_ref, inc_ref, loss_ref, out_ref, all_ref):
    is_last = lax.axis_index("pipe") == lax.axis_size("pipe") - 1
    all_ref[...] = rows_ref[...]
    for half in range(2):
        lanes = slice(half * BLOCK, (half + 1) * BLOCK)
        grad = jnp.where(is_last, loss_ref[:, lanes].astype(F32), inc_ref[:, lanes].astype(F32))
        all_ref[pl.ds(6 + half, BLOCK, stride=ROWS), :] = grad.T
    out_ref[...] = all_ref[...].astype(BF16)


def to_spectrum(high, low, gather, turn, mix):
    part = dot(gather[0], high) + dot(gather[1], high)
    if low is not None:
        part = part + dot(gather[0], low)
    real, imag = (part[:BLOCK], part[BLOCK:])
    turned_re = real * turn[0] - imag * turn[1]
    turned_im = real * turn[1] + imag * turn[0]
    stacked = jnp.concatenate(
        [
            jnp.concatenate([turned_re[:, :BLOCK], turned_im[:, :BLOCK]], axis=1),
            jnp.concatenate([turned_re[:, BLOCK:], turned_im[:, BLOCK:]], axis=1),
        ],
        axis=0,
    )
    return dot3(split(stacked), mix)


def main_kernel(
    in_ref, gh_ref, gl_ref, ah_ref, al_ref, tr_ref, ti_ref, mh_ref, ml_ref, bh_ref, bl_ref, sh_ref, sl_ref, out_ref, rows_ref, back_ref
):
    gather = (gh_ref[...], gl_ref[...])
    is_moved = lax.axis_index("pipe") == 1
    moved = (jnp.where(is_moved, ah_ref[...], gather[0]), jnp.where(is_moved, al_ref[...], gather[1]))
    turn = (tr_ref[...], ti_ref[...])
    mix = (mh_ref[...], ml_ref[...])
    back = (bh_ref[...], bl_ref[...])
    spread = (sh_ref[...], sl_ref[...])
    rows_ref[...] = in_ref[...].astype(F32)

    def pair(r):
        both = [rows_ref[pl.ds(r + half, BLOCK, stride=ROWS), :].astype(BF16) for half in range(2)]
        return jnp.concatenate(both, axis=1)

    grad = to_spectrum(pair(6), None, moved, turn, mix)
    g_re, g_im = (grad[:, :BLOCK], grad[:, BLOCK:])
    taps = to_spectrum(pair(2), pair(4), gather, turn, mix)
    inputs = to_spectrum(pair(0), None, gather, turn, mix)
    for index, other in enumerate((taps, inputs)):
        o_re, o_im = (other[:, :BLOCK], other[:, BLOCK:])
        product = jnp.concatenate([o_re * g_re + o_im * g_im, o_re * g_im - o_im * g_re], axis=1)
        part = dot3(split(product), back)
        real = jnp.concatenate([part[:BLOCK, :BLOCK], part[BLOCK:, :BLOCK]], axis=1)
        imag = jnp.concatenate([part[:BLOCK, BLOCK:], part[BLOCK:, BLOCK:]], axis=1)
        stacked = jnp.concatenate([real * turn[0] + imag * turn[1], imag * turn[0] - real * turn[1]], axis=0)
        value = dot3(spread, split(stacked))
        for half in range(2):
            one = value[:, half * BLOCK : (half + 1) * BLOCK]
            if index == 0:
                back_ref[pl.ds(half, BLOCK, stride=BACK_ROWS), :] = one
            else:
                one = one * (1.0 / math.sqrt(LENGTH))
                high = one.astype(BF16).astype(F32)
                back_ref[pl.ds(2 + half, BLOCK, stride=BACK_ROWS), :] = high
                back_ref[pl.ds(4 + half, BLOCK, stride=BACK_ROWS), :] = one - high
    out_ref[...] = back_ref[...].astype(BF16)


def unpack_kernel(in_ref, grad_ref, filt_ref, rows_ref):
    rows_ref[...] = in_ref[...].astype(F32)
    for half in range(2):
        lanes = slice(half * BLOCK, (half + 1) * BLOCK)
        grad_ref[:, lanes] = rows_ref[pl.ds(half, BLOCK, stride=BACK_ROWS), :].T.astype(BF16)
        both = rows_ref[pl.ds(2 + half, BLOCK, stride=BACK_ROWS), :] + rows_ref[pl.ds(4 + half, BLOCK, stride=BACK_ROWS), :]
        filt_ref[:, lanes] = both.T


def shape(rows, columns, kind):
    return jax.ShapeDtypeStruct((rows, columns), kind)


def near(value):
    return pltpu.with_memory_space_constraint(value, pltpu.VMEM)


def call(kernel, outs, ins, scratch=()):
    return pl.pallas_call(
        kernel,
        out_shape=outs,
        in_specs=[VMEM] * ins,
        out_specs=jax.tree.map(lambda _: VMEM, outs),
        scratch_shapes=scratch,
    )


ROW_SCRATCH = (pltpu.VMEM((ROWS * BLOCK, BLOCK), F32),)
BACK_SCRATCH = (pltpu.VMEM((BACK_ROWS * BLOCK, BLOCK), F32),)
WIDE = 2 * BLOCK


def packed_rows(rows):
    return pltpu.VMEM((rows * BLOCK, BLOCK), BF16)


def exchanged(packed):
    rows = packed.shape[0] // BLOCK
    block = (rows, BLOCK) if rows % 8 == 0 else (rows // 2, 2, BLOCK)
    blocks = packed.reshape(BLOCK, *block)
    blocks = lax.all_to_all(blocks, "seq", split_axis=0, concat_axis=0, tiled=True, axis_index_groups=[ORDER])
    return near(blocks.reshape(packed.shape))


def route():
    parts = lax.axis_size("pipe")
    devices = lax.axis_size("seq")
    return [(p * devices + q, (p - 1) * devices + (q ^ 2 if p == 2 else q)) for p in range(1, parts) for q in range(devices)]


def per_device(layer_input, filters, skip, incoming, loss_grad):
    constants = [near(jnp.asarray(half)) for pair in tables() for half in pair]
    passed = lax.ppermute(incoming[0], ("pipe", "seq"), route())
    rows = call(pack_kernel, pltpu.VMEM((ROWS * BLOCK, BLOCK), F32), 3)(layer_input[0], filters[0], skip)
    packed = call(join_kernel, packed_rows(ROWS), 3, ROW_SCRATCH)(near(rows), near(passed), near(loss_grad))
    results = call(main_kernel, packed_rows(BACK_ROWS), 13, ROW_SCRATCH + BACK_SCRATCH)(exchanged(packed), *constants)
    outs = (shape(BLOCK, WIDE, BF16), shape(BLOCK, WIDE, F32))
    input_grad, filter_grad = call(unpack_kernel, outs, 1, BACK_SCRATCH)(exchanged(results))
    return (input_grad[None], filter_grad[None])


def solution(mesh):
    return jax.shard_map(
        per_device,
        mesh=mesh,
        in_specs=(
            P("pipe", "seq", None),
            P("pipe", "seq", None),
            P("pipe", None),
            P("pipe", "seq", None),
            P("seq", None),
        ),
        out_specs=(P("pipe", "seq", None), P("pipe", "seq", None)),
        check_vma=False,
    )
```

```python
import math

import jax
import jax.numpy as jnp
import numpy as np
from jax import lax
from jax.experimental import pallas as pl
from jax.experimental.pallas import tpu as pltpu
from jax.sharding import PartitionSpec as P

BF16 = jnp.bfloat16
F32 = jnp.float32
BLOCK = 128
LENGTH = BLOCK * BLOCK
ROWS = 8
BACK_ROWS = 6
ORDER = [int(f"{i:07b}"[::-1], 2) for i in range(BLOCK)]
VMEM = pl.BlockSpec(memory_space=pltpu.VMEM)
SMEM = pl.BlockSpec(memory_space=pltpu.SMEM)
SENT_FROM = (3, 2, 0, 1)


def halves(table):
    high = table.astype(BF16)
    low = (table - high.astype(np.float64)).astype(BF16)
    return (high, low)


def tables():
    q = np.arange(BLOCK)
    order = np.array(ORDER)
    first = 2.0 * math.pi * np.outer(q + 0.25, order) / BLOCK
    sent = order - order % 4 + np.array(SENT_FROM)[order % 4]
    moved = 2.0 * math.pi * np.outer(q + 0.25, sent) / BLOCK
    twist = 2.0 * math.pi * np.outer(q + 0.25, q) / LENGTH
    second = 2.0 * math.pi * (np.outer(q, q) % BLOCK) / BLOCK
    gather = np.concatenate([np.cos(first), -np.sin(first)], axis=0)
    moved = np.concatenate([np.cos(moved), -np.sin(moved)], axis=0)
    turn_re = np.tile(np.cos(twist), (1, 2)).astype(np.float32)
    turn_im = np.tile(-np.sin(twist), (1, 2)).astype(np.float32)
    cos, sin = (np.cos(second), -np.sin(second))
    mix = np.block([[cos, sin], [-sin, cos]])
    spread = gather.T / LENGTH
    return (halves(gather), halves(moved), (turn_re, turn_im), halves(mix), halves(mix.T), halves(spread))


def split(value):
    high = value.astype(BF16)
    return (high, (value - high.astype(F32)).astype(BF16))


def dot(left, right):
    return jnp.dot(left, right, preferred_element_type=F32)


def dot3(left, right):
    return dot(left[0], right[0]) + dot(left[0], right[1]) + dot(left[1], right[0])


def pack_kernel(x_ref, f_ref, skip_ref, rows_ref):
    at_start = jnp.where(lax.axis_index("seq") == 0, 1.0, 0.0)
    row = lax.broadcasted_iota(jnp.int32, (BLOCK, BLOCK), 0)
    first_row = jnp.where(row == 0, at_start, 0.0)
    for half in range(2):
        lanes = slice(half * BLOCK, (half + 1) * BLOCK)
        rows_ref[pl.ds(half, BLOCK, stride=ROWS), :] = x_ref[:, lanes].astype(F32).T
        taps = (f_ref[:, lanes] + first_row * skip_ref[:, lanes]).T
        high = taps.astype(BF16).astype(F32)
        rows_ref[pl.ds(2 + half, BLOCK, stride=ROWS), :] = high
        rows_ref[pl.ds(4 + half, BLOCK, stride=ROWS), :] = taps - high


def join_kernel(rows_ref, far_ref, near_ref, loss_ref, out_ref, all_ref):
    pipe = lax.axis_index("pipe")
    all_ref[...] = rows_ref[...]
    for half in range(2):
        lanes = slice(half * BLOCK, (half + 1) * BLOCK)
        grad = jnp.where(pipe == 1, far_ref[:, lanes].astype(F32), near_ref[:, lanes].astype(F32))
        grad = jnp.where(pipe == 3, loss_ref[:, lanes].astype(F32), grad)
        all_ref[pl.ds(6 + half, BLOCK, stride=ROWS), :] = grad.T
    out_ref[...] = all_ref[...].astype(BF16)


def to_spectrum(high, low, gather, turn, mix):
    part = dot(gather[0], high) + dot(gather[1], high)
    if low is not None:
        part = part + dot(gather[0], low)
    real, imag = (part[:BLOCK], part[BLOCK:])
    turned_re = real * turn[0] - imag * turn[1]
    turned_im = real * turn[1] + imag * turn[0]
    stacked = jnp.concatenate(
        [
            jnp.concatenate([turned_re[:, :BLOCK], turned_im[:, :BLOCK]], axis=1),
            jnp.concatenate([turned_re[:, BLOCK:], turned_im[:, BLOCK:]], axis=1),
        ],
        axis=0,
    )
    return dot3(split(stacked), mix)


def main_kernel(
    in_ref, gh_ref, gl_ref, ah_ref, al_ref, tr_ref, ti_ref, mh_ref, ml_ref, bh_ref, bl_ref, sh_ref, sl_ref, out_ref, rows_ref, back_ref
):
    gather = (gh_ref[...], gl_ref[...])
    is_moved = lax.axis_index("pipe") == 1
    moved = (jnp.where(is_moved, ah_ref[...], gather[0]), jnp.where(is_moved, al_ref[...], gather[1]))
    turn = (tr_ref[...], ti_ref[...])
    mix = (mh_ref[...], ml_ref[...])
    back = (bh_ref[...], bl_ref[...])
    spread = (sh_ref[...], sl_ref[...])
    rows_ref[...] = in_ref[...].astype(F32)

    def pair(r):
        both = [rows_ref[pl.ds(r + half, BLOCK, stride=ROWS), :].astype(BF16) for half in range(2)]
        return jnp.concatenate(both, axis=1)

    grad = to_spectrum(pair(6), None, moved, turn, mix)
    g_re, g_im = (grad[:, :BLOCK], grad[:, BLOCK:])
    taps = to_spectrum(pair(2), pair(4), gather, turn, mix)
    inputs = to_spectrum(pair(0), None, gather, turn, mix)
    for index, other in enumerate((taps, inputs)):
        o_re, o_im = (other[:, :BLOCK], other[:, BLOCK:])
        product = jnp.concatenate([o_re * g_re + o_im * g_im, o_re * g_im - o_im * g_re], axis=1)
        part = dot3(split(product), back)
        real = jnp.concatenate([part[:BLOCK, :BLOCK], part[BLOCK:, :BLOCK]], axis=1)
        imag = jnp.concatenate([part[:BLOCK, BLOCK:], part[BLOCK:, BLOCK:]], axis=1)
        stacked = jnp.concatenate([real * turn[0] + imag * turn[1], imag * turn[0] - real * turn[1]], axis=0)
        value = dot3(spread, split(stacked))
        for half in range(2):
            one = value[:, half * BLOCK : (half + 1) * BLOCK]
            if index == 0:
                back_ref[pl.ds(half, BLOCK, stride=BACK_ROWS), :] = one
            else:
                one = one * (1.0 / math.sqrt(LENGTH))
                high = one.astype(BF16).astype(F32)
                back_ref[pl.ds(2 + half, BLOCK, stride=BACK_ROWS), :] = high
                back_ref[pl.ds(4 + half, BLOCK, stride=BACK_ROWS), :] = one - high
    out_ref[...] = back_ref[...].astype(BF16)


def unpack_kernel(in_ref, grad_ref, filt_ref, rows_ref):
    rows_ref[...] = in_ref[...].astype(F32)
    for half in range(2):
        lanes = slice(half * BLOCK, (half + 1) * BLOCK)
        grad_ref[:, lanes] = rows_ref[pl.ds(half, BLOCK, stride=BACK_ROWS), :].T.astype(BF16)
        both = rows_ref[pl.ds(2 + half, BLOCK, stride=BACK_ROWS), :] + rows_ref[pl.ds(4 + half, BLOCK, stride=BACK_ROWS), :]
        filt_ref[:, lanes] = both.T


def shape(rows, columns, kind):
    return jax.ShapeDtypeStruct((rows, columns), kind)


def near(value):
    return pltpu.with_memory_space_constraint(value, pltpu.VMEM)


def call(kernel, outs, ins, scratch=()):
    return pl.pallas_call(
        kernel,
        out_shape=outs,
        in_specs=[VMEM] * ins,
        out_specs=jax.tree.map(lambda _: VMEM, outs),
        scratch_shapes=scratch,
    )


ROW_SCRATCH = (pltpu.VMEM((ROWS * BLOCK, BLOCK), F32),)
BACK_SCRATCH = (pltpu.VMEM((BACK_ROWS * BLOCK, BLOCK), F32),)
WIDE = 2 * BLOCK


def packed_rows(rows):
    return pltpu.VMEM((rows * BLOCK, BLOCK), BF16)


def exchanged(packed):
    rows = packed.shape[0] // BLOCK
    block = (rows, BLOCK) if rows % 8 == 0 else (rows // 2, 2, BLOCK)
    blocks = packed.reshape(BLOCK, *block)
    blocks = lax.all_to_all(blocks, "seq", split_axis=0, concat_axis=0, tiled=True, axis_index_groups=[ORDER])
    return near(blocks.reshape(packed.shape))


def far_route():
    devices = lax.axis_size("seq")
    from_of = [q - q % 4 + SENT_FROM[q % 4] for q in range(devices)]
    return [(2 * devices + from_of[q], devices + q) for q in range(devices)]


def per_device(layer_input, filters, skip, incoming, loss_grad):
    constants = [near(jnp.asarray(half)) for pair in tables() for half in pair]
    far = lax.ppermute(incoming[0], ("pipe", "seq"), far_route())
    passed = lax.ppermute(incoming[0], "pipe", [(1, 0), (3, 2)])
    rows = call(pack_kernel, pltpu.VMEM((ROWS * BLOCK, BLOCK), F32), 3)(layer_input[0], filters[0], skip)
    packed = call(join_kernel, packed_rows(ROWS), 4, ROW_SCRATCH)(near(rows), near(far), near(passed), near(loss_grad))
    results = call(main_kernel, packed_rows(BACK_ROWS), 13, ROW_SCRATCH + BACK_SCRATCH)(exchanged(packed), *constants)
    outs = (shape(BLOCK, WIDE, BF16), shape(BLOCK, WIDE, F32))
    input_grad, filter_grad = call(unpack_kernel, outs, 1, BACK_SCRATCH)(exchanged(results))
    return (input_grad[None], filter_grad[None])


def solution(mesh):
    return jax.shard_map(
        per_device,
        mesh=mesh,
        in_specs=(
            P("pipe", "seq", None),
            P("pipe", "seq", None),
            P("pipe", None),
            P("pipe", "seq", None),
            P("seq", None),
        ),
        out_specs=(P("pipe", "seq", None), P("pipe", "seq", None)),
        check_vma=False,
    )
```

```python
import math
import random

import jax
import jax.numpy as jnp
import numpy as np
from jax import lax
from jax.experimental import pallas as pl
from jax.experimental.pallas import tpu as pltpu
from jax.sharding import PartitionSpec as P

BF16 = jnp.bfloat16
F32 = jnp.float32
BLOCK = 128
LENGTH = BLOCK * BLOCK
ROWS = 8
BACK_ROWS = 6
ORDER = list(range(BLOCK))
random.Random(17).shuffle(ORDER)
WIDE = 2 * BLOCK
HALVES = (slice(0, BLOCK), slice(BLOCK, WIDE))
VMEM = pl.BlockSpec(memory_space=pltpu.VMEM)
SENT_FROM = (3, 2, 0, 1)


def halves(table):
    high = table.astype(BF16)
    low = (table - high.astype(np.float64)).astype(BF16)
    return (high, low)


def beside(table):
    high, low = halves(table)
    return np.concatenate([high, low, high], axis=1)


def stacked(table):
    high, low = halves(table)
    return np.concatenate([high, low, high], axis=0)


def tables():
    q = np.arange(BLOCK)
    order = np.array(ORDER)
    first = 2.0 * math.pi * np.outer(q + 0.25, order) / BLOCK
    sent = order - order % 4 + np.array(SENT_FROM)[order % 4]
    moved = 2.0 * math.pi * np.outer(q + 0.25, sent) / BLOCK
    twist = 2.0 * math.pi * np.outer(q + 0.25, q) / LENGTH
    second = 2.0 * math.pi * (np.outer(q, q) % BLOCK) / BLOCK
    gather = np.concatenate([np.cos(first), -np.sin(first)], axis=0)
    moved = np.concatenate([np.cos(moved), -np.sin(moved)], axis=0)
    turn_re = np.tile(np.cos(twist), (1, 2)).astype(np.float32)
    turn_im = np.tile(-np.sin(twist), (1, 2)).astype(np.float32)
    cos, sin = (np.cos(second), -np.sin(second))
    mix = np.block([[cos, sin], [-sin, cos]])
    spread = gather.T / LENGTH
    return (beside(gather), np.stack([beside(t)[:, :WIDE] for t in (gather, moved)]), turn_re, turn_im, stacked(mix), stacked(mix.T), beside(spread))


def split(value):
    high = value.astype(BF16)
    return (high, (value - high.astype(F32)).astype(BF16))


def dot(left, right):
    return jnp.dot(left, right, preferred_element_type=F32)


def pack_kernel(x_ref, f_ref, skip_ref, rows_ref):
    at_start = jnp.where(lax.axis_index("seq") == 0, 1.0, 0.0)
    row = lax.broadcasted_iota(jnp.int32, (BLOCK, BLOCK), 0)
    first_row = jnp.where(row == 0, at_start, 0.0)
    for half in range(2):
        lanes = slice(half * BLOCK, (half + 1) * BLOCK)
        rows_ref[pl.ds(half, BLOCK, stride=ROWS), :] = x_ref[:, lanes].astype(F32).T
        taps = (f_ref[:, lanes] + first_row * skip_ref[:, lanes]).T
        high = taps.astype(BF16).astype(F32)
        rows_ref[pl.ds(2 + half, BLOCK, stride=ROWS), :] = high
        rows_ref[pl.ds(4 + half, BLOCK, stride=ROWS), :] = taps - high


def join_kernel(rows_ref, far_ref, near_ref, loss_ref, out_ref, all_ref):
    pipe = lax.axis_index("pipe")
    all_ref[...] = rows_ref[...]
    for half in range(2):
        lanes = slice(half * BLOCK, (half + 1) * BLOCK)
        grad = jnp.where(pipe == 1, far_ref[:, lanes].astype(F32), near_ref[:, lanes].astype(F32))
        grad = jnp.where(pipe == 3, loss_ref[:, lanes].astype(F32), grad)
        all_ref[pl.ds(6 + half, BLOCK, stride=ROWS), :] = grad.T
    out_ref[...] = all_ref[...].astype(BF16)


def turned_rows(part, turn):
    real, imag = (part[:BLOCK], part[BLOCK:])
    turned_re = real * turn[0] - imag * turn[1]
    turned_im = real * turn[1] + imag * turn[0]
    rows = [jnp.concatenate([turned_re[:, lanes], turned_im[:, lanes]], axis=1) for lanes in HALVES]
    return jnp.concatenate(rows, axis=0)


def thrice(value):
    high, low = split(value)
    return jnp.concatenate([high, high, low], axis=1)


def main_kernel(
    in_ref, gather_ref, moved_ref, tr_ref, ti_ref, mix_ref, back_ref, spread_ref, out_ref, rows_ref, store_ref
):
    turn = (tr_ref[...], ti_ref[...])
    rows_ref[...] = in_ref[...].astype(F32)

    def pair(r):
        both = [rows_ref[pl.ds(r + half, BLOCK, stride=ROWS), :].astype(BF16) for half in range(2)]
        return jnp.concatenate(both, axis=1)

    gather = gather_ref[...]
    moved = moved_ref[jnp.where(lax.axis_index("pipe") == 1, 1, 0)]
    grad, high, low, inputs = (pair(6), pair(2), pair(4), pair(0))
    parts = (
        dot(moved, jnp.concatenate([grad, grad], axis=0)),
        dot(gather[:, :WIDE], jnp.concatenate([inputs, inputs], axis=0)),
        dot(gather, jnp.concatenate([high, high, low], axis=0)),
    )
    left = [turned_rows(part, turn) for part in parts]
    grad, inputs, taps = [dot(thrice(rows), mix_ref[...]) for rows in left]
    g_re, g_im = (grad[:, :BLOCK], grad[:, BLOCK:])
    products = []
    for other in (inputs, taps):
        o_re, o_im = (other[:, :BLOCK], other[:, BLOCK:])
        products.append(jnp.concatenate([o_re * g_re + o_im * g_im, o_re * g_im - o_im * g_re], axis=1))
    parts = [dot(thrice(product), back_ref[...]) for product in products]
    sides = []
    for part in parts:
        real = jnp.concatenate([part[:BLOCK, :BLOCK], part[BLOCK:, :BLOCK]], axis=1)
        imag = jnp.concatenate([part[:BLOCK, BLOCK:], part[BLOCK:, BLOCK:]], axis=1)
        above, below = split(jnp.concatenate([real * turn[0] + imag * turn[1], imag * turn[0] - real * turn[1]], axis=0))
        sides.append(jnp.concatenate([above, above, below], axis=0))
    of_filter, of_input = [dot(spread_ref[...], side) for side in sides]
    for half, lanes in enumerate(HALVES):
        one = of_filter[:, lanes] * (1.0 / math.sqrt(LENGTH))
        head = one.astype(BF16).astype(F32)
        store_ref[pl.ds(2 + half, BLOCK, stride=BACK_ROWS), :] = head
        store_ref[pl.ds(4 + half, BLOCK, stride=BACK_ROWS), :] = one - head
        store_ref[pl.ds(half, BLOCK, stride=BACK_ROWS), :] = of_input[:, lanes]
    out_ref[...] = store_ref[...].astype(BF16)


def unpack_kernel(in_ref, grad_ref, filt_ref, rows_ref, grad_near, filt_near, sems):
    rows_ref[...] = in_ref[...].astype(F32)
    copies = []
    for half, lanes in enumerate(HALVES):
        both = rows_ref[pl.ds(2 + half, BLOCK, stride=BACK_ROWS), :] + rows_ref[pl.ds(4 + half, BLOCK, stride=BACK_ROWS), :]
        filt_near[:, lanes] = both.T
        copies.append(pltpu.make_async_copy(filt_near.at[:, lanes], filt_ref.at[:, lanes], sems.at[half]))
        copies[-1].start()
    for half, lanes in enumerate(HALVES):
        grad_near[:, lanes] = rows_ref[pl.ds(half, BLOCK, stride=BACK_ROWS), :].T.astype(BF16)
        copies.append(pltpu.make_async_copy(grad_near.at[:, lanes], grad_ref.at[:, lanes], sems.at[2 + half]))
        copies[-1].start()
    for copy in copies:
        copy.wait()


def shape(rows, columns, kind):
    return jax.ShapeDtypeStruct((rows, columns), kind)


def near(value):
    return pltpu.with_memory_space_constraint(value, pltpu.VMEM)


def call(kernel, outs, ins, scratch=(), to=VMEM):
    return pl.pallas_call(
        kernel,
        out_shape=outs,
        in_specs=[VMEM] * ins,
        out_specs=jax.tree.map(lambda _: to, outs),
        scratch_shapes=scratch,
    )


ROW_SCRATCH = (pltpu.VMEM((ROWS * BLOCK, BLOCK), F32),)
BACK_SCRATCH = (pltpu.VMEM((BACK_ROWS * BLOCK, BLOCK), F32),)
OUT_SCRATCH = (
    *BACK_SCRATCH,
    pltpu.VMEM((BLOCK, WIDE), BF16),
    pltpu.VMEM((BLOCK, WIDE), F32),
    pltpu.SemaphoreType.DMA((4,)),
)
MAIN_SCRATCH = (*ROW_SCRATCH, *BACK_SCRATCH)


def packed_rows(rows):
    return pltpu.VMEM((rows * BLOCK, BLOCK), BF16)


def exchanged(packed):
    rows = packed.shape[0] // BLOCK
    block = (rows, BLOCK) if rows % 8 == 0 else (rows // 2, 2, BLOCK)
    blocks = packed.reshape(BLOCK, *block)
    blocks = lax.all_to_all(blocks, "seq", split_axis=0, concat_axis=0, tiled=True, axis_index_groups=[ORDER])
    return near(blocks.reshape(packed.shape))


def far_route():
    devices = lax.axis_size("seq")
    from_of = [q - q % 4 + SENT_FROM[q % 4] for q in range(devices)]
    return [(2 * devices + from_of[q], devices + q) for q in range(devices)]


def per_device(layer_input, filters, skip, incoming, loss_grad):
    constants = [near(jnp.asarray(table)) for table in tables()]
    far = lax.ppermute(incoming[0], ("pipe", "seq"), far_route())
    passed = lax.ppermute(incoming[0], "pipe", [(1, 0), (3, 2)])
    rows = call(pack_kernel, pltpu.VMEM((ROWS * BLOCK, BLOCK), F32), 3)(layer_input[0], filters[0], skip)
    packed = call(join_kernel, packed_rows(ROWS), 4, ROW_SCRATCH)(near(rows), near(far), near(passed), near(loss_grad))
    results = call(main_kernel, packed_rows(BACK_ROWS), 8, MAIN_SCRATCH)(exchanged(packed), *constants)
    outs = (shape(BLOCK, WIDE, BF16), shape(BLOCK, WIDE, F32))
    input_grad, filter_grad = call(unpack_kernel, outs, 1, OUT_SCRATCH, pl.BlockSpec(memory_space=pl.ANY))(exchanged(results))
    return (input_grad[None], filter_grad[None])


def solution(mesh):
    return jax.shard_map(
        per_device,
        mesh=mesh,
        in_specs=(
            P("pipe", "seq", None),
            P("pipe", "seq", None),
            P("pipe", None),
            P("pipe", "seq", None),
            P("seq", None),
        ),
        out_specs=(P("pipe", "seq", None), P("pipe", "seq", None)),
        check_vma=False,
    )
```
